32 devices in a mesh: seq: 8 (over z, y), head: 4 (over x, core).
Axes of the slice: x: 2, y: 2, z: 4, core: 2. Of those that a mesh axis runs over, the one named last changes fastest.
Arguments:
- mel_buffer: bfloat16 [16384, 128], P('seq'), may hold values from -6 to 6
- segment_frames: int32 [64], P('seq'), may hold values from 0 to 2048, as said below
- conv1_weight: bfloat16 [3, 128, 1280], replicated, may hold values from -0.3125 to 0.3125
- conv1_bias: float32 [1280], replicated, may hold values from -3 to 3
- conv2_weight: bfloat16 [3, 1280, 1280], P(None, 'seq', 'head'), may hold values from -0.09375 to 0.09375
- conv2_bias: float32 [1280], P('head'), may hold values from -3 to 3
- norm_gain: float32 [1280], replicated, may hold values from 0.1 to 1.9
- norm_bias: float32 [1280], replicated, may hold values from -3 to 3
- qkv_weight: bfloat16 [1280, 3840], P('seq', 'head'), may hold values from -0.15625 to 0.15625
Outputs:
- qkv: bfloat16 [4096, 3840], P('seq', 'head')
The draws below stay inside these ranges and needn't reach their ends.
Inputs may be any that keep to these rules, and one draw needn't show every extreme that they name: `segment_frames`: with S_i the sum of the counts of blocks 0 to i, S_i - (i + 1) * 1024 lies in 0 to 1024 and is 0 for the last block; the counts of one block add to at most 2048, and those of some block add to exactly 2048, all of them in one segment of that block, its other segments being empty.
All inputs are finite; a program needn't handle non-finite values.
Results may differ from the reference program's by a relative error of at most 0.006.
Values may be sent and summed in bfloat16 or wider, within the bound.
A program may use at most 128 MiB of HBM per device.

```python
import math
import jax
import jax.numpy as jnp
from jax import lax

WIDTH = 1280
MELS = 128
CONTEXT = 1500
SEGMENTS = 8
FRAMES_DEV = 1024
BUFFER = 2048
TOK_DEV = 512
FRAMES = 8192
TOKENS = 4096
QKV_WIDTH = 3840
N_SEQ = 8


def draw_segment_frames(key, part):
    key_drift = jax.random.fold_in(key, 11)
    key_pick = jax.random.fold_in(key, 12)
    key_cuts = jax.random.fold_in(key, 13)
    device_ids = jnp.arange(N_SEQ, dtype=jnp.int32)
    displaced = jax.random.randint(key_drift, (N_SEQ,), 0, FRAMES_DEV + 1, dtype=jnp.int32)
    chosen = jax.random.randint(key_pick, (), 1, N_SEQ - 1, dtype=jnp.int32)
    displaced = jnp.where(device_ids == chosen, FRAMES_DEV, displaced)
    displaced = jnp.where(device_ids == chosen - 1, 0, displaced)
    displaced = jnp.where(device_ids == N_SEQ - 1, 0, displaced)
    earlier = jnp.concatenate([jnp.zeros((1,), jnp.int32), displaced[:-1]])
    counts = (FRAMES_DEV + displaced - earlier).astype(jnp.int32)
    raw_cuts = jax.random.randint(key_cuts, (N_SEQ, SEGMENTS - 1), 0, 65536, dtype=jnp.int32)
    cut_rows = raw_cuts * (counts[:, None] + 1) // 65536
    cut_rows = jnp.where((device_ids == chosen)[:, None], 0, cut_rows).astype(jnp.int32)
    cut_rows = jnp.sort(cut_rows, axis=1)
    edges = jnp.concatenate([jnp.zeros((N_SEQ, 1), jnp.int32), cut_rows, counts[:, None]], axis=1)
    return (edges[:, 1:] - edges[:, :-1]).reshape(-1).astype(jnp.int32)


def levels(key, dims, pieces, least, high):
    def one(position, shards_of):
        heights = jax.random.uniform(jax.random.fold_in(jax.random.fold_in(key, 6), position), (shards_of,), jnp.float32, least / len(pieces), high / len(pieces))
        return jnp.repeat(jnp.exp(heights), dims[position] // shards_of).reshape((-1,) + (1,) * (len(dims) - position - 1))

    factor_of = one(*pieces[0])
    for cut in pieces[1:]:
        factor_of = factor_of * one(*cut)
    return factor_of


def noise(own_key, extent, scale, bound, cuts=(), kind=jnp.bfloat16):
    values = scale * jax.random.normal(own_key, extent, jnp.float32)
    if cuts:
        values = values * levels(own_key, extent, cuts, -0.22, 0.18)
    return jnp.clip(values, -bound, bound).astype(kind)


def setup_inputs(seed: int = 0) -> dict:
    arg_keys = jax.random.split(jax.random.key(seed), 10)
    mel_buffer = noise(arg_keys[0], (N_SEQ * BUFFER, MELS), 1.0, 6.0, ((0, 8),))
    segment_frames = draw_segment_frames(jax.random.fold_in(arg_keys[9], 71), 0)
    conv1_weight = noise(arg_keys[2], (3, MELS, WIDTH), (3 * MELS) ** -0.5, 0.3125)
    conv1_bias = noise(arg_keys[3], (WIDTH,), 0.5, 3.0, (), jnp.float32)
    conv2_weight = noise(arg_keys[4], (3, WIDTH, WIDTH), (3 * WIDTH) ** -0.5, 0.09375, ((1, 8), (2, 4)))
    conv2_bias = noise(arg_keys[5], (WIDTH,), 0.5, 3.0, ((0, 4),), jnp.float32)
    norm_gain = jnp.clip(1.0 + 0.18 * jax.random.normal(arg_keys[6], (WIDTH,), jnp.float32), 0.1, 1.9)
    norm_bias = noise(arg_keys[7], (WIDTH,), 0.5, 3.0, (), jnp.float32)
    qkv_weight = noise(arg_keys[8], (WIDTH, QKV_WIDTH), WIDTH ** -0.5, 0.15625, ((0, 8), (1, 4)))
    return dict(mel_buffer=mel_buffer, segment_frames=segment_frames, conv1_weight=conv1_weight, conv1_bias=conv1_bias, conv2_weight=conv2_weight, conv2_bias=conv2_bias, norm_gain=norm_gain, norm_bias=norm_bias, qkv_weight=qkv_weight)


LOG_SCALE = math.log(10000.0)

def sinusoid(token_ids, channel_ids, width_all):
    half_width = width_all // 2
    inv_rate = jnp.exp(-(LOG_SCALE / (half_width - 1)) * (channel_ids % half_width).astype(jnp.float32))
    angles = (token_ids % CONTEXT).astype(jnp.float32)[:, None] * inv_rate[None, :]
    return jnp.where(channel_ids[None, :] < half_width, jnp.sin(angles), jnp.cos(angles))

def layer_norm(values, gain, shift):
    widened = values.astype(jnp.float32)
    average = lax.optimization_barrier(jnp.mean(widened, axis=-1, keepdims=True))
    centered = widened - average
    spread = lax.optimization_barrier(jnp.mean(centered * centered, axis=-1, keepdims=True))
    return (centered * lax.rsqrt(spread + 1e-05) * gain + shift).astype(jnp.bfloat16)

def reference(mel_buffer, segment_frames, conv1_weight, conv1_bias, conv2_weight, conv2_bias, norm_gain, norm_bias, qkv_weight):
    counts = lax.optimization_barrier(jnp.sum(segment_frames.reshape(N_SEQ, SEGMENTS), axis=1)).astype(jnp.int32)
    starts = (jnp.cumsum(counts) - counts).astype(jnp.int32)
    row_ids = jnp.arange(BUFFER, dtype=jnp.int32)
    target = starts[:, None] + row_ids[None, :]
    target = jnp.where(row_ids[None, :] < counts[:, None], target, FRAMES).astype(jnp.int32)
    stream = jnp.zeros((FRAMES + 1, MELS), jnp.bfloat16).at[target.reshape(-1)].set(mel_buffer)[:FRAMES]
    padded = jnp.pad(stream, ((2, 1), (0, 0)))
    channel = jnp.arange(WIDTH, dtype=jnp.int32)

    def one_block(block_index):
        offset = (block_index * FRAMES_DEV).astype(jnp.int32)
        window = lax.dynamic_slice_in_dim(padded, offset, FRAMES_DEV + 3, 0)
        running = jnp.zeros((FRAMES_DEV + 1, WIDTH), jnp.float32)
        for k in range(3):
            running = running + jnp.dot(window[k:k + FRAMES_DEV + 1], conv1_weight[k], preferred_element_type=jnp.float32)
        first_layer = jax.nn.gelu(running + conv1_bias, approximate=False).astype(jnp.bfloat16)
        frame_ids = offset - 1 + jnp.arange(FRAMES_DEV + 1, dtype=jnp.int32)
        first_layer = jnp.where((frame_ids >= 0)[:, None], first_layer, jnp.zeros_like(first_layer))
        frame_pairs = first_layer[:FRAMES_DEV].reshape(TOK_DEV, 2, WIDTH)
        later_pairs = first_layer[1:].reshape(TOK_DEV, 2, WIDTH)
        conv_taps = (frame_pairs[:, 0], frame_pairs[:, 1], later_pairs[:, 1])
        stem_sum = jnp.zeros((TOK_DEV, WIDTH), jnp.float32)
        for k in range(3):
            stem_sum = stem_sum + jnp.dot(conv_taps[k], conv2_weight[k], preferred_element_type=jnp.float32)
        token_ids = (block_index * TOK_DEV).astype(jnp.int32) + jnp.arange(TOK_DEV, dtype=jnp.int32)
        stem = (jax.nn.gelu(stem_sum + conv2_bias, approximate=False) + sinusoid(token_ids, channel, WIDTH)).astype(jnp.bfloat16)
        normed = layer_norm(stem, norm_gain, norm_bias)
        return jnp.dot(normed, qkv_weight, preferred_element_type=jnp.float32).astype(jnp.bfloat16)
    blocks = lax.map(one_block, jnp.arange(N_SEQ, dtype=jnp.int32))
    return blocks.reshape(TOKENS, QKV_WIDTH)
```

```python
import functools
import math

import jax
import jax.numpy as jnp
from jax import lax
from jax.experimental import pallas as pl
from jax.experimental.pallas import tpu as pltpu
from jax.sharding import PartitionSpec as P

CONTEXT = 1500


LOG_SCALE = math.log(10000.0)


def prefix(value, axis, join, neutral):
    count, mine = (lax.axis_size(axis), lax.axis_index(axis))
    pieces = lax.all_gather(value, axis)
    running = jnp.full_like(value, 0) + jnp.asarray(neutral, value.dtype)

    def step(position, running):
        longer = join(running, pieces[position])
        return jnp.where(position < mine, longer, running)

    return lax.fori_loop(0, count - 1, step, running)


def from_behind(value, axis, by):
    size = lax.axis_size(axis)
    pairs = [(i, i + by) for i in range(size) if 0 <= i + by < size]
    return lax.ppermute(value, axis, pairs)


def padded(value, sides, width):
    for axis, dim in sides:
        size, length = (lax.axis_size(axis), value.shape[dim])
        up = [(i, (i + 1) % size) for i in range(size - 1)]
        down = [(j, i) for i, j in up]
        last = lax.slice_in_dim(value, length - width, length, axis=dim)
        initial = lax.slice_in_dim(value, 0, width, axis=dim)
        before = lax.ppermute(last, axis, up)
        after = lax.ppermute(initial, axis, down)
        value = jnp.concatenate([before, value, after], axis=dim)
    return value


def sinusoid(token_ids, channel_ids, width_all):
    half_width = width_all // 2
    inv_rate = jnp.exp(
        -(LOG_SCALE / (half_width - 1)) * (channel_ids % half_width).astype(jnp.float32)
    )
    angles = (token_ids % CONTEXT).astype(jnp.float32)[:, None] * inv_rate[None, :]
    return jnp.where(channel_ids[None, :] < half_width, jnp.sin(angles), jnp.cos(angles))


def layer_norm(values, gain, shift):
    widened = values.astype(jnp.float32)
    average = jnp.mean(widened, axis=-1, keepdims=True)
    centered = widened - average
    spread = jnp.mean(centered * centered, axis=-1, keepdims=True)
    return (centered * lax.rsqrt(spread + 1e-05) * gain + shift).astype(jnp.bfloat16)


def add_sum(left, right):
    return left + right


def project_rows(normed, shard_rows):
    return jnp.dot(normed, shard_rows, preferred_element_type=jnp.float32)


def per_device(
    mel_buffer,
    segment_frames,
    conv1_weight,
    conv1_bias,
    conv2_weight,
    conv2_bias,
    norm_gain,
    norm_bias,
    qkv_weight,
):
    frames_dev = mel_buffer.shape[0] // 2
    tok_rows = frames_dev // 2
    width_all = conv1_weight.shape[2]
    seq_place = lax.axis_index("seq")
    head_place = lax.axis_index("head")
    own_count = jnp.sum(segment_frames)
    start_frame = prefix(own_count, "seq", add_sum, jnp.zeros((), jnp.int32))
    displaced = (start_frame - seq_place * frames_dev).astype(jnp.int32)
    tail_rows = lax.dynamic_slice_in_dim(mel_buffer, frames_dev - displaced, frames_dev, 0)
    arrived = from_behind(tail_rows, "seq", 1)
    front_pad = jnp.concatenate([jnp.zeros_like(arrived), mel_buffer[:frames_dev]], axis=0)
    own_rows = lax.dynamic_slice_in_dim(front_pad, frames_dev - displaced, frames_dev, 0)
    row_ids = jnp.arange(frames_dev, dtype=jnp.int32)
    frames = jnp.where((row_ids < displaced)[:, None], arrived, own_rows)
    rimmed = padded(frames, (("seq", 0),), 2)
    running = jnp.zeros((frames_dev + 1, width_all), jnp.float32)
    for k in range(3):
        running = running + jnp.dot(
            rimmed[k : k + frames_dev + 1], conv1_weight[k], preferred_element_type=jnp.float32
        )
    first_layer = jax.nn.gelu(running + conv1_bias, approximate=False).astype(jnp.bfloat16)
    keep_mask = (jnp.arange(frames_dev + 1, dtype=jnp.int32) > 0) | (seq_place > 0)
    first_layer = jnp.where(keep_mask[:, None], first_layer, jnp.zeros_like(first_layer))
    frame_pairs = first_layer[:frames_dev].reshape(tok_rows, 2, width_all)
    later_pairs = first_layer[1:].reshape(tok_rows, 2, width_all)
    conv_taps = (frame_pairs[:, 0], frame_pairs[:, 1], later_pairs[:, 1])
    quarter_width = conv2_weight.shape[2]
    zero_start = jnp.zeros((tok_rows, quarter_width), jnp.float32)
    stem_sum = zero_start
    shard_rows = lax.all_gather(conv2_weight, "seq", axis=1, tiled=True)
    for k in range(3):
        inputs = conv_taps[k]
        stem_sum = stem_sum + jnp.dot(inputs, shard_rows[k], preferred_element_type=jnp.float32)
    token_ids = seq_place * tok_rows + jnp.arange(tok_rows, dtype=jnp.int32)
    channel = head_place * quarter_width + jnp.arange(quarter_width, dtype=jnp.int32)
    features = (
        jax.nn.gelu(stem_sum + conv2_bias, approximate=False)
        + sinusoid(token_ids, channel, width_all)
    ).astype(jnp.bfloat16)
    quarter = lax.all_to_all(features, "head", split_axis=0, concat_axis=1, tiled=True)
    normed = layer_norm(quarter, norm_gain, norm_bias)
    widened_rows = lax.all_gather(qkv_weight, "head", axis=1, tiled=True)
    qkv_part = project_rows(normed, lax.all_gather(widened_rows, "seq", axis=0, tiled=True))
    return lax.all_to_all(
        qkv_part.astype(jnp.bfloat16), "head", split_axis=1, concat_axis=0, tiled=True
    )


MESH = pl.DeviceIdType.MESH
HALO = 16
Y_FIRST = (2,)


def gelu(v):
    return 0.5 * v * (1.0 + lax.erf(v * math.sqrt(0.5)))


def fused_kernel(
    dims, seg_ref, mel_ref, w1_ref, b1_ref, w2_ref, b2_ref, gain_ref, shift_ref, wq_ref,
    out_ref, seg_all, tail_send, tail_recv, fr, halo_prev, halo_next, ebuf, obuf, x_even, x_odd,
    f_even, f_odd, w2g, wqg, stem, acc0, seg_s, seg_r, tail_s, tail_r, halo_s, halo_r,
    w_s, w_r, loc, st_s, st_r,
):
    n, depth, width_all, quarter = dims
    nz = n // 2
    toks = fr.shape[1]
    frames_dev = 2 * toks
    me = lax.axis_index("seq")
    h = lax.axis_index("head")
    z, y = me // 2, me % 2
    partner = z * 2 + (1 - y)
    f32, bf16 = jnp.float32, jnp.bfloat16
    pending = []

    def remote(src, dst, ss, rs, axis, peer):
        return pltpu.make_async_remote_copy(
            src_ref=src, dst_ref=dst, send_sem=ss, recv_sem=rs,
            device_id={axis: peer}, device_id_type=MESH,
        )

    def start(cond, copy):
        if cond is None:
            copy.start()
        else:
            pl.when(cond)(copy.start)
        pending.append((cond, copy))

    def both(a, b):
        if a is None:
            return b
        return a if b is None else jnp.logical_and(a, b)

    barrier = pltpu.get_barrier_semaphore()
    for p in range(1, n):
        pl.semaphore_signal(
            barrier, inc=1, device_id={"seq": lax.rem(me + p, n)}, device_id_type=MESH
        )
    for p in range(1, 4):
        pl.semaphore_signal(
            barrier, inc=1, device_id={"head": lax.rem(h + p, 4)}, device_id_type=MESH
        )
    pl.semaphore_wait(barrier, n - 1 + 3)

    for p in range(1, n):
        dst = lax.rem(me + p, n)
        start(None, remote(seg_ref, seg_all.at[me], seg_s.at[p], seg_r.at[me], "seq", dst))

    half = depth // 2

    def gathered(p, s):
        if p < 3:
            return w2g.at[p, pl.ds(pl.multiple_of(s * depth, 16), depth), :]
        return wqg.at[pl.ds(pl.multiple_of(s * depth + (p - 3) * half, 16), half), :]

    def own(p):
        return w2_ref.at[p] if p < 3 else wq_ref.at[pl.ds((p - 3) * half, half), :]

    has_up, has_down = z < nz - 1, z > 0

    def push(cond, p, s, way, mine=False):
        peer = (lax.rem(me + 2, n), lax.rem(me + n - 2, n), partner)[way]
        src = own(p) if mine else gathered(p, s)
        start(cond, remote(src, gathered(p, s), w_s.at[p, s, way], w_r.at[p, s], "seq", peer))

    def arrive(cond, p, s):
        copy = remote(gathered(p, s), gathered(p, s), w_s.at[p, s, 0], w_r.at[p, s], "seq", partner)
        if cond is None:
            copy.wait_recv()
        else:
            pl.when(cond)(copy.wait_recv)

    def start_own(p):
        push(None, p, me, 2, True)
        push(has_up, p, me, 0, True)
        push(has_down, p, me, 1, True)
        pltpu.make_async_copy(own(p), gathered(p, me), loc.at[p]).start()

    def relay_partner(p):
        if p in Y_FIRST:
            arrive(None, p, partner)
            push(has_up, p, partner, 0)
            push(has_down, p, partner, 1)

    def relay(p, k):
        for way in (0, 1):
            valid = z - k >= 0 if way == 0 else z + k <= nz - 1
            onward = has_up if way == 0 else has_down
            shift = -2 * k if way == 0 else 2 * k
            for base in (me, partner) if p in Y_FIRST else (me,):
                s = lax.rem(base + shift + 2 * n, n)
                arrive(valid, p, s)
                push(both(valid, onward), p, s, way)
                if p not in Y_FIRST:
                    push(valid, p, s, 2)

    def finish(p):
        if p not in Y_FIRST:
            for q in range(nz):
                arrive(None, p, 2 * q + (1 - y))
        pltpu.make_async_copy(own(p), gathered(p, me), loc.at[p]).wait()

    for p in (2, 0, 1):
        start_own(p)

    total = jnp.zeros((8, 128), f32)
    for p in range(1, n):
        src = lax.rem(me + n - p, n)
        remote(seg_ref, seg_all.at[src], seg_s.at[p], seg_r.at[src], "seq", src).wait_recv()
        total = total + jnp.where(src < me, seg_all[src].astype(f32), 0.0)
    total = jnp.sum(jnp.sum(total, axis=1, keepdims=True), axis=0, keepdims=True)
    moved = total.astype(jnp.int32) - me * frames_dev

    rows = 128

    def shifted(first, parity, depth_rows):
        frame = 2 * (first + lax.broadcasted_iota(jnp.int32, (rows, depth_rows), 0)) + parity
        column = lax.broadcasted_iota(jnp.int32, (rows, depth_rows), 1)
        pick = jnp.where(frame - column == moved, 1.0, 0.0).astype(bf16)
        return jnp.dot(pick, mel_ref[:depth_rows, :], preferred_element_type=f32)

    for parity in (0, 1):
        def tail_step(i, c):
            at = pl.multiple_of(i * rows, rows)
            tail_send[parity, pl.ds(at, rows), :] = shifted(
                toks + at, parity, 2 * frames_dev
            ).astype(bf16)
            return c
        lax.fori_loop(0, toks // rows, tail_step, 0)
        start(me < n - 1, remote(
            tail_send.at[parity], tail_recv.at[parity], tail_s.at[parity], tail_r.at[parity],
            "seq", lax.rem(me + 1, n)))

    relay_partner(2)

    for parity, buf in ((0, ebuf), (1, obuf)):
        def own_step(i, c):
            at = pl.multiple_of(i * rows, rows)
            buf[pl.ds(HALO + at, rows), :] = shifted(at, parity, frames_dev)
            return c
        lax.fori_loop(0, toks // rows, own_step, 0)

    for parity, buf in ((0, ebuf), (1, obuf)):
        copy = remote(
            tail_send.at[parity], tail_recv.at[parity], tail_s.at[parity], tail_r.at[parity],
            "seq", lax.rem(me + 1, n))
        pl.when(me > 0)(copy.wait_recv)
        frame = 2 * lax.broadcasted_iota(jnp.int32, (toks, 128), 0) + parity
        joined = jnp.where(
            frame < moved, tail_recv[parity].astype(f32), buf[HALO : HALO + toks, :])
        buf[HALO : HALO + toks, :] = joined
        fr[parity] = joined.astype(bf16)

    nxt, prv = lax.rem(me + 1, n), lax.rem(me + n - 1, n)
    halos = [
        (me < n - 1, me > 0, fr.at[0, pl.ds(toks - HALO, HALO), :], halo_prev.at[0], nxt),
        (me < n - 1, me > 0, fr.at[1, pl.ds(toks - HALO, HALO), :], halo_prev.at[1], nxt),
        (me > 0, me < n - 1, fr.at[0, pl.ds(0, HALO), :], halo_next, prv),
    ]
    copies = [remote(s, d, halo_s.at[i], halo_r.at[i], "seq", peer)
              for i, (_, _, s, d, peer) in enumerate(halos)]
    for (sends, _, _, _, _), copy in zip(halos, copies):
        start(sends, copy)

    for p in (2, 0, 1):
        relay(p, 1)

    x_even[:, 128:256] = fr[0]
    x_even[:, 256:384] = fr[1]

    for (_, takes, _, _, _), copy in zip(halos, copies):
        pl.when(takes)(copy.wait_recv)
    ebuf[0:HALO, :] = jnp.where(me > 0, halo_prev[0].astype(f32), 0.0)
    obuf[0:HALO, :] = jnp.where(me > 0, halo_prev[1].astype(f32), 0.0)
    ebuf[HALO + toks :, :] = jnp.where(me < n - 1, halo_next[...].astype(f32), 0.0)
    x_even[:, 0:128] = obuf[HALO - 1 : HALO - 1 + toks, :].astype(bf16)
    x_odd[:, 0:128] = ebuf[0 : HALO + toks, :].astype(bf16)
    x_odd[:, 128:256] = obuf[0 : HALO + toks, :].astype(bf16)
    x_odd[:, 256:384] = ebuf[1 : HALO + toks + 1, :].astype(bf16)

    start_own(3)
    start_own(4)

    cols = 256

    def even_step(i, c):
        at = pl.ds(pl.multiple_of(i * cols, cols), cols)
        acc = jnp.dot(x_even[...], w1_ref[:, at], preferred_element_type=f32)
        f_even[:, at] = gelu(acc + b1_ref[:, at]).astype(bf16)
        return c

    def odd_step(i, c):
        at = pl.ds(pl.multiple_of(i * cols, cols), cols)
        acc = jnp.dot(x_odd[...], w1_ref[:, at], preferred_element_type=f32)
        f_odd[:, at] = gelu(acc + b1_ref[:, at]).astype(bf16)
        return c

    lax.fori_loop(0, width_all // cols, even_step, 0)
    for p in (2, 0, 1):
        relay(p, 2)
    lax.fori_loop(0, width_all // cols, odd_step, 0)
    keep = jnp.where(me > 0, f_odd[0:HALO, :].astype(f32), 0.0)
    f_odd[0:HALO, :] = keep.astype(bf16)
    for p in (3, 4):
        relay(p, 1)
    for p in (2, 0, 1):
        for k in range(3, nz):
            relay(p, k)
    for p in (3, 4):
        relay(p, 2)
    for p in (2, 0, 1):
        finish(p)

    odd_rows = (HALO + toks) // 3

    def tap_zero(i, c):
        at = pl.ds(pl.multiple_of(i * odd_rows, 16), odd_rows)
        acc0[at, :] = jnp.dot(f_odd[at, :], w2g[0], preferred_element_type=f32)
        return c

    lax.fori_loop(0, 3, tap_zero, 0)
    half_width = width_all // 2
    lane = lax.broadcasted_iota(jnp.int32, (1, quarter), 1) + lax.rem(h * quarter, half_width)
    rate = jnp.exp(-(LOG_SCALE / (half_width - 1)) * lane.astype(f32))
    first_token = lax.rem(me * toks, CONTEXT)
    for i in range(toks // rows):
        acc = jnp.dot(f_even[i * rows : (i + 1) * rows, :], w2g[1], preferred_element_type=f32)
        acc = acc + jnp.dot(
            f_odd[HALO + i * rows : HALO + (i + 1) * rows, :], w2g[2], preferred_element_type=f32)
        acc = acc + acc0[HALO - 1 + i * rows : HALO - 1 + (i + 1) * rows, :]
        token = first_token + i * rows + lax.broadcasted_iota(jnp.int32, (rows, 1), 0)
        token = jnp.where(token >= CONTEXT, token - CONTEXT, token)
        angle = token.astype(f32) * rate
        place = jnp.where(h * quarter < half_width, jnp.sin(angle), jnp.cos(angle))
        stem[h, i * rows : (i + 1) * rows, :] = (gelu(acc + b2_ref[...]) + place).astype(bf16)

    core_peer = (h // 2) * 2 + (1 - h % 2)
    x_peer = lax.rem(h + 2, 4)
    far = lax.rem(core_peer + 2, 4)
    start(None, remote(stem.at[h], stem.at[h], st_s.at[0], st_r.at[0], "head", x_peer))
    start(None, remote(stem.at[h], stem.at[h], st_s.at[1], st_r.at[1], "head", core_peer))
    for p in (3, 4):
        for k in range(3, nz):
            relay(p, k)
    remote(stem.at[x_peer], stem.at[x_peer], st_s.at[0], st_r.at[0], "head", x_peer).wait_recv()
    start(None, remote(stem.at[x_peer], stem.at[x_peer], st_s.at[2], st_r.at[2], "head", core_peer))
    remote(stem.at[core_peer], stem.at[core_peer], st_s.at[1], st_r.at[1], "head", core_peer).wait_recv()
    remote(stem.at[far], stem.at[far], st_s.at[2], st_r.at[2], "head", core_peer).wait_recv()
    for p in (3, 4):
        finish(p)

    def project(i, c):
        at = pl.ds(pl.multiple_of(i * rows, rows), rows)
        parts = [stem[j, at, :].astype(f32) for j in range(4)]
        mean = sum(jnp.sum(v, axis=1, keepdims=True) for v in parts) / width_all
        parts = [v - mean for v in parts]
        var = sum(jnp.sum(v * v, axis=1, keepdims=True) for v in parts) / width_all
        scale = lax.rsqrt(var + 1e-05)
        acc = None
        for j in range(4):
            lanes = slice(j * quarter, (j + 1) * quarter)
            normed = (parts[j] * scale * gain_ref[:, lanes] + shift_ref[:, lanes]).astype(bf16)
            term = jnp.dot(normed, wqg[lanes, :], preferred_element_type=f32)
            acc = term if acc is None else acc + term
        out_ref[at, :] = acc.astype(bf16)
        return c

    lax.fori_loop(0, toks // rows, project, 0)

    for cond, copy in pending:
        if cond is None:
            copy.wait_send()
        else:
            pl.when(cond)(copy.wait_send)


def fused_device(
    n, mel_buffer, segment_frames, conv1_weight, conv1_bias, conv2_weight, conv2_bias,
    norm_gain, norm_bias, qkv_weight,
):
    toks = mel_buffer.shape[0] // 4
    taps, mels, width_all = conv1_weight.shape
    depth, quarter = conv2_weight.shape[1:]
    out_cols = qkv_weight.shape[1]
    bf16, f32 = jnp.bfloat16, jnp.float32
    seg = jnp.pad(segment_frames[None, :], ((0, 7), (0, 128 - segment_frames.shape[0])))
    vmem = pl.BlockSpec(memory_space=pltpu.VMEM)
    dma = pltpu.SemaphoreType.DMA
    return pl.pallas_call(
        functools.partial(fused_kernel, (n, depth, width_all, quarter)),
        out_shape=jax.ShapeDtypeStruct((toks, out_cols), bf16),
        in_specs=[vmem] * 9,
        out_specs=vmem,
        scratch_shapes=[
            pltpu.VMEM((n, 8, 128), jnp.int32),
            pltpu.VMEM((2, toks, 128), bf16),
            pltpu.VMEM((2, toks, 128), bf16),
            pltpu.VMEM((2, toks, 128), bf16),
            pltpu.VMEM((2, HALO, 128), bf16),
            pltpu.VMEM((HALO, 128), bf16),
            pltpu.VMEM((toks + 2 * HALO, 128), f32),
            pltpu.VMEM((toks + 2 * HALO, 128), f32),
            pltpu.VMEM((toks, 384), bf16),
            pltpu.VMEM((toks + HALO, 384), bf16),
            pltpu.VMEM((toks, width_all), bf16),
            pltpu.VMEM((toks + HALO, width_all), bf16),
            pltpu.VMEM((3, width_all, quarter), bf16),
            pltpu.VMEM((width_all, out_cols), bf16),
            pltpu.VMEM((4, toks, quarter), bf16),
            pltpu.VMEM((toks + HALO, quarter), f32),
            dma((n,)), dma((n,)), dma((2,)), dma((2,)), dma((3,)), dma((3,)),
            dma((5, n, 3)), dma((5, n)), dma((5,)), dma((3,)), dma((3,)),
        ],
        compiler_params=pltpu.CompilerParams(
            collective_id=0, has_side_effects=True, vmem_limit_bytes=60 * 1024 * 1024
        ),
    )(
        seg, mel_buffer, conv1_weight.reshape(taps * mels, width_all), conv1_bias[None, :],
        conv2_weight, conv2_bias[None, :], norm_gain[None, :], norm_bias[None, :], qkv_weight,
    )


def solution(mesh):
    n_seq, n_head = mesh.shape["seq"], mesh.shape["head"]

    def local(*args):
        depth = args[4].shape[1]
        if n_head == 4 and n_seq % 2 == 0 and depth % 32 == 0:
            return fused_device(n_seq, *args)
        return per_device(*args)

    in_specs = (
        P("seq", None),
        P("seq"),
        P(),
        P(),
        P(None, "seq", "head"),
        P("head"),
        P(),
        P(),
        P("seq", "head"),
    )
    out_specs = P("seq", "head")
    return jax.shard_map(
        local, mesh=mesh, in_specs=in_specs, out_specs=out_specs, check_vma=False
    )
```

```python
import functools
import math

import jax
import jax.numpy as jnp
from jax import lax
from jax.experimental import pallas as pl
from jax.experimental.pallas import tpu as pltpu
from jax.sharding import PartitionSpec as P

CONTEXT = 1500


LOG_SCALE = math.log(10000.0)


def prefix(value, axis, join, neutral):
    count, mine = (lax.axis_size(axis), lax.axis_index(axis))
    pieces = lax.all_gather(value, axis)
    running = jnp.full_like(value, 0) + jnp.asarray(neutral, value.dtype)

    def step(position, running):
        longer = join(running, pieces[position])
        return jnp.where(position < mine, longer, running)

    return lax.fori_loop(0, count - 1, step, running)


def from_behind(value, axis, by):
    size = lax.axis_size(axis)
    pairs = [(i, i + by) for i in range(size) if 0 <= i + by < size]
    return lax.ppermute(value, axis, pairs)


def padded(value, sides, width):
    for axis, dim in sides:
        size, length = (lax.axis_size(axis), value.shape[dim])
        up = [(i, (i + 1) % size) for i in range(size - 1)]
        down = [(j, i) for i, j in up]
        last = lax.slice_in_dim(value, length - width, length, axis=dim)
        initial = lax.slice_in_dim(value, 0, width, axis=dim)
        before = lax.ppermute(last, axis, up)
        after = lax.ppermute(initial, axis, down)
        value = jnp.concatenate([before, value, after], axis=dim)
    return value


def sinusoid(token_ids, channel_ids, width_all):
    half_width = width_all // 2
    inv_rate = jnp.exp(
        -(LOG_SCALE / (half_width - 1)) * (channel_ids % half_width).astype(jnp.float32)
    )
    angles = (token_ids % CONTEXT).astype(jnp.float32)[:, None] * inv_rate[None, :]
    return jnp.where(channel_ids[None, :] < half_width, jnp.sin(angles), jnp.cos(angles))


def layer_norm(values, gain, shift):
    widened = values.astype(jnp.float32)
    average = jnp.mean(widened, axis=-1, keepdims=True)
    centered = widened - average
    spread = jnp.mean(centered * centered, axis=-1, keepdims=True)
    return (centered * lax.rsqrt(spread + 1e-05) * gain + shift).astype(jnp.bfloat16)


def add_sum(left, right):
    return left + right


def project_rows(normed, shard_rows):
    return jnp.dot(normed, shard_rows, preferred_element_type=jnp.float32)


def per_device(
    mel_buffer,
    segment_frames,
    conv1_weight,
    conv1_bias,
    conv2_weight,
    conv2_bias,
    norm_gain,
    norm_bias,
    qkv_weight,
):
    frames_dev = mel_buffer.shape[0] // 2
    tok_rows = frames_dev // 2
    width_all = conv1_weight.shape[2]
    seq_place = lax.axis_index("seq")
    head_place = lax.axis_index("head")
    own_count = jnp.sum(segment_frames)
    start_frame = prefix(own_count, "seq", add_sum, jnp.zeros((), jnp.int32))
    displaced = (start_frame - seq_place * frames_dev).astype(jnp.int32)
    tail_rows = lax.dynamic_slice_in_dim(mel_buffer, frames_dev - displaced, frames_dev, 0)
    arrived = from_behind(tail_rows, "seq", 1)
    front_pad = jnp.concatenate([jnp.zeros_like(arrived), mel_buffer[:frames_dev]], axis=0)
    own_rows = lax.dynamic_slice_in_dim(front_pad, frames_dev - displaced, frames_dev, 0)
    row_ids = jnp.arange(frames_dev, dtype=jnp.int32)
    frames = jnp.where((row_ids < displaced)[:, None], arrived, own_rows)
    rimmed = padded(frames, (("seq", 0),), 2)
    running = jnp.zeros((frames_dev + 1, width_all), jnp.float32)
    for k in range(3):
        running = running + jnp.dot(
            rimmed[k : k + frames_dev + 1], conv1_weight[k], preferred_element_type=jnp.float32
        )
    first_layer = jax.nn.gelu(running + conv1_bias, approximate=False).astype(jnp.bfloat16)
    keep_mask = (jnp.arange(frames_dev + 1, dtype=jnp.int32) > 0) | (seq_place > 0)
    first_layer = jnp.where(keep_mask[:, None], first_layer, jnp.zeros_like(first_layer))
    frame_pairs = first_layer[:frames_dev].reshape(tok_rows, 2, width_all)
    later_pairs = first_layer[1:].reshape(tok_rows, 2, width_all)
    conv_taps = (frame_pairs[:, 0], frame_pairs[:, 1], later_pairs[:, 1])
    quarter_width = conv2_weight.shape[2]
    zero_start = jnp.zeros((tok_rows, quarter_width), jnp.float32)
    stem_sum = zero_start
    shard_rows = lax.all_gather(conv2_weight, "seq", axis=1, tiled=True)
    for k in range(3):
        inputs = conv_taps[k]
        stem_sum = stem_sum + jnp.dot(inputs, shard_rows[k], preferred_element_type=jnp.float32)
    token_ids = seq_place * tok_rows + jnp.arange(tok_rows, dtype=jnp.int32)
    channel = head_place * quarter_width + jnp.arange(quarter_width, dtype=jnp.int32)
    features = (
        jax.nn.gelu(stem_sum + conv2_bias, approximate=False)
        + sinusoid(token_ids, channel, width_all)
    ).astype(jnp.bfloat16)
    quarter = lax.all_to_all(features, "head", split_axis=0, concat_axis=1, tiled=True)
    normed = layer_norm(quarter, norm_gain, norm_bias)
    widened_rows = lax.all_gather(qkv_weight, "head", axis=1, tiled=True)
    qkv_part = project_rows(normed, lax.all_gather(widened_rows, "seq", axis=0, tiled=True))
    return lax.all_to_all(
        qkv_part.astype(jnp.bfloat16), "head", split_axis=1, concat_axis=0, tiled=True
    )


MESH = pl.DeviceIdType.MESH
HALO = 16
Y_FIRST = (2,)


def gelu(v):
    return 0.5 * v * (1.0 + lax.erf(v * math.sqrt(0.5)))


def fused_kernel(
    dims, vec_ref, mel_ref, w1_ref, w2_ref, wq_ref,
    out_ref, seg_all, tail_send, tail_recv, fr, halo_prev, halo_next, ebuf, obuf, x_even, x_odd,
    f_even, f_odd, w2g, wqg, rest, restg, stem, acc0, seg_s, seg_r, tail_s, tail_r, halo_s, halo_r,
    w_s, w_r, loc, st_s, st_r,
):
    n, depth, width_all, quarter = dims
    nz = n // 2
    toks = fr.shape[1]
    frames_dev = 2 * toks
    me = lax.axis_index("seq")
    h = lax.axis_index("head")
    z, y = me // 2, me % 2
    partner = z * 2 + (1 - y)
    f32, bf16 = jnp.float32, jnp.bfloat16
    core = h % 2
    core_peer = (h // 2) * 2 + (1 - core)
    seg_ref = vec_ref.at[pl.ds(8, 8), pl.ds(0, 128)]
    pending = []

    def remote(src, dst, ss, rs, axis, peer):
        return pltpu.make_async_remote_copy(
            src_ref=src, dst_ref=dst, send_sem=ss, recv_sem=rs,
            device_id={axis: peer}, device_id_type=MESH,
        )

    def start(cond, copy):
        if cond is None:
            copy.start()
        else:
            pl.when(cond)(copy.start)
        pending.append((cond, copy))

    def both(a, b):
        if a is None:
            return b
        return a if b is None else jnp.logical_and(a, b)

    barrier = pltpu.get_barrier_semaphore()
    for p in range(1, n):
        pl.semaphore_signal(
            barrier, inc=1, device_id={"seq": lax.rem(me + p, n)}, device_id_type=MESH
        )
    for p in range(1, 4):
        pl.semaphore_signal(
            barrier, inc=1, device_id={"head": lax.rem(h + p, 4)}, device_id_type=MESH
        )
    pl.semaphore_wait(barrier, n - 1 + 3)

    for p in range(1, n):
        dst = lax.rem(me + p, n)
        start(None, remote(seg_ref, seg_all.at[me], seg_s.at[p], seg_r.at[me], "seq", dst))

    half = depth // 2
    out_cols = wqg.shape[1]
    main2, main_q = quarter - 64, out_cols - 64
    lanes2, lanes_q = pl.ds(0, main2), pl.ds(0, main_q)

    def gathered(p, s):
        if p < 3:
            return w2g.at[p, pl.ds(pl.multiple_of(s * depth, 16), depth), lanes2]
        if p == 5:
            return restg.at[s]
        return wqg.at[pl.ds(pl.multiple_of(s * depth + (p - 3) * half, 16), half), lanes_q]

    def own(p):
        if p == 5:
            return rest
        return w2_ref.at[p, :, lanes2] if p < 3 else wq_ref.at[pl.ds((p - 3) * half, half), lanes_q]

    has_up, has_down = z < nz - 1, z > 0

    def push(cond, p, s, way, mine=False):
        peer = (lax.rem(me + 2, n), lax.rem(me + n - 2, n), partner)[way]
        src = own(p) if mine else gathered(p, s)
        start(cond, remote(src, gathered(p, s), w_s.at[p, s, way], w_r.at[p, s], "seq", peer))

    def arrive(cond, p, s):
        copy = remote(gathered(p, s), gathered(p, s), w_s.at[p, s, 0], w_r.at[p, s], "seq", partner)
        if cond is None:
            copy.wait_recv()
        else:
            pl.when(cond)(copy.wait_recv)

    def start_own(p):
        push(None, p, me, 2, True)
        push(has_up, p, me, 0, True)
        push(has_down, p, me, 1, True)
        pltpu.make_async_copy(own(p), gathered(p, me), loc.at[p]).start()

    def relay_partner(p):
        if p in Y_FIRST:
            arrive(None, p, partner)
            push(has_up, p, partner, 0)
            push(has_down, p, partner, 1)

    def relay(p, k):
        for way in (0, 1):
            valid = z - k >= 0 if way == 0 else z + k <= nz - 1
            onward = has_up if way == 0 else has_down
            shift = -2 * k if way == 0 else 2 * k
            for base in (me, partner) if p in Y_FIRST else (me,):
                s = lax.rem(base + shift + 2 * n, n)
                arrive(valid, p, s)
                push(both(valid, onward), p, s, way)
                if p not in Y_FIRST:
                    push(valid, p, s, 2)

    def finish(p):
        if p not in Y_FIRST:
            for q in range(nz):
                arrive(None, p, 2 * q + (1 - y))
        pltpu.make_async_copy(own(p), gathered(p, me), loc.at[p]).wait()

    early = (2, 5, 0, 1)
    start_own(2)
    rest[0:depth, 0:64] = w2_ref[0, :, main2:]
    rest[0:depth, 64:128] = w2_ref[1, :, main2:]
    rest[depth : depth + half, 0:64] = w2_ref[2, 0:half, main2:]
    rest[depth : depth + half, 64:128] = w2_ref[2, half:, main2:]
    rest[depth + half :, 0:64] = wq_ref[0:half, main_q:]
    rest[depth + half :, 64:128] = wq_ref[half:, main_q:]
    for p in early[1:]:
        start_own(p)

    total = jnp.zeros((8, 128), f32)
    for p in range(1, n):
        src = lax.rem(me + n - p, n)
        remote(seg_ref, seg_all.at[src], seg_s.at[p], seg_r.at[src], "seq", src).wait_recv()
        total = total + jnp.where(src < me, seg_all[src], 0.0)
    total = jnp.sum(jnp.sum(total, axis=1, keepdims=True), axis=0, keepdims=True)
    moved = total.astype(jnp.int32) - me * frames_dev

    rows = 128

    def shifted(first, parity, depth_rows):
        frame = 2 * (first + lax.broadcasted_iota(jnp.int32, (rows, depth_rows), 0)) + parity
        column = lax.broadcasted_iota(jnp.int32, (rows, depth_rows), 1)
        pick = jnp.where(frame - column == moved, 1.0, 0.0).astype(bf16)
        return jnp.dot(pick, mel_ref[:depth_rows, :], preferred_element_type=f32)

    def tail_step(i, c):
        at = pl.multiple_of(i * rows, rows)
        tail_send[pl.ds(at, rows), :] = shifted(toks + at, core, 2 * frames_dev).astype(bf16)
        return c

    lax.fori_loop(0, toks // rows, tail_step, 0)
    tail = remote(tail_send, tail_recv.at[core], tail_s.at[0], tail_r.at[core],
                  "seq", lax.rem(me + 1, n))
    start(me < n - 1, tail)

    relay_partner(2)

    for parity, buf in ((0, ebuf), (1, obuf)):
        def own_step(i, c):
            at = pl.multiple_of(i * rows, rows)
            buf[pl.ds(HALO + at, rows), :] = shifted(at, parity, frames_dev)
            return c
        lax.fori_loop(0, toks // rows, own_step, 0)

    pl.when(me > 0)(tail.wait_recv)
    start(me > 0, remote(tail_recv.at[core], tail_recv.at[core], tail_s.at[1], tail_r.at[core],
                         "head", core_peer))
    pl.when(me > 0)(remote(
        tail_recv.at[1 - core], tail_recv.at[1 - core], tail_s.at[1], tail_r.at[1 - core],
        "head", core_peer).wait_recv)
    for parity, buf in ((0, ebuf), (1, obuf)):
        frame = 2 * lax.broadcasted_iota(jnp.int32, (toks, 128), 0) + parity
        joined = jnp.where(
            frame < moved, tail_recv[parity].astype(f32), buf[HALO : HALO + toks, :])
        buf[HALO : HALO + toks, :] = joined
        fr[parity] = joined.astype(bf16)

    nxt, prv = lax.rem(me + 1, n), lax.rem(me + n - 1, n)
    halos = [
        (me < n - 1, me > 0, fr.at[0, pl.ds(toks - HALO, HALO), :], halo_prev.at[0], nxt),
        (me < n - 1, me > 0, fr.at[1, pl.ds(toks - HALO, HALO), :], halo_prev.at[1], nxt),
        (me > 0, me < n - 1, fr.at[0, pl.ds(0, HALO), :], halo_next, prv),
    ]
    copies = [remote(s, d, halo_s.at[i], halo_r.at[i], "seq", peer)
              for i, (_, _, s, d, peer) in enumerate(halos)]
    for (sends, _, _, _, _), copy in zip(halos, copies):
        start(sends, copy)

    for p in early:
        relay(p, 1)

    x_even[:, 128:256] = fr[0]
    x_even[:, 256:384] = fr[1]

    for (_, takes, _, _, _), copy in zip(halos, copies):
        pl.when(takes)(copy.wait_recv)
    ebuf[0:HALO, :] = jnp.where(me > 0, halo_prev[0].astype(f32), 0.0)
    obuf[0:HALO, :] = jnp.where(me > 0, halo_prev[1].astype(f32), 0.0)
    ebuf[HALO + toks :, :] = jnp.where(me < n - 1, halo_next[...].astype(f32), 0.0)
    x_even[:, 0:128] = obuf[HALO - 1 : HALO - 1 + toks, :].astype(bf16)
    x_odd[:, 0:128] = ebuf[0 : HALO + toks, :].astype(bf16)
    x_odd[:, 128:256] = obuf[0 : HALO + toks, :].astype(bf16)
    x_odd[:, 256:384] = ebuf[1 : HALO + toks + 1, :].astype(bf16)

    start_own(3)
    start_own(4)

    cols = 256

    def even_step(i, c):
        at = pl.ds(pl.multiple_of(i * cols, cols), cols)
        acc = jnp.dot(x_even[...], w1_ref[:, at], preferred_element_type=f32)
        f_even[:, at] = gelu(acc + vec_ref[0:1, at]).astype(bf16)
        return c

    def odd_step(i, c):
        at = pl.ds(pl.multiple_of(i * cols, cols), cols)
        acc = jnp.dot(x_odd[...], w1_ref[:, at], preferred_element_type=f32)
        f_odd[:, at] = gelu(acc + vec_ref[0:1, at]).astype(bf16)
        return c

    lax.fori_loop(0, width_all // cols, even_step, 0)
    for p in early:
        relay(p, 2)
    lax.fori_loop(0, width_all // cols, odd_step, 0)
    keep = jnp.where(me > 0, f_odd[0:HALO, :].astype(f32), 0.0)
    f_odd[0:HALO, :] = keep.astype(bf16)
    for p in (3, 4):
        relay(p, 1)
    for p in early:
        for k in range(3, nz):
            relay(p, k)
    for p in (3, 4):
        relay(p, 2)
    for p in early:
        finish(p)

    for j in range(n):
        at = slice(j * depth, (j + 1) * depth)
        w2g[0, at, main2:] = restg[j, 0:depth, 0:64]
        w2g[1, at, main2:] = restg[j, 0:depth, 64:128]
        w2g[2, j * depth : j * depth + half, main2:] = restg[j, depth : depth + half, 0:64]
        w2g[2, j * depth + half : (j + 1) * depth, main2:] = restg[j, depth : depth + half, 64:128]
        wqg[j * depth : j * depth + half, main_q:] = restg[j, depth + half :, 0:64]
        wqg[j * depth + half : (j + 1) * depth, main_q:] = restg[j, depth + half :, 64:128]

    odd_rows = (HALO + toks) // 3

    def tap_zero(i, c):
        at = pl.ds(pl.multiple_of(i * odd_rows, 16), odd_rows)
        acc0[at, :] = jnp.dot(f_odd[at, :], w2g[0], preferred_element_type=f32)
        return c

    lax.fori_loop(0, 3, tap_zero, 0)
    half_width = width_all // 2
    lane = lax.broadcasted_iota(jnp.int32, (1, quarter), 1) + lax.rem(h * quarter, half_width)
    rate = jnp.exp(-(LOG_SCALE / (half_width - 1)) * lane.astype(f32))
    first_token = lax.rem(me * toks, CONTEXT)
    for i in range(toks // rows):
        acc = jnp.dot(f_even[i * rows : (i + 1) * rows, :], w2g[1], preferred_element_type=f32)
        acc = acc + jnp.dot(
            f_odd[HALO + i * rows : HALO + (i + 1) * rows, :], w2g[2], preferred_element_type=f32)
        acc = acc + acc0[HALO - 1 + i * rows : HALO - 1 + (i + 1) * rows, :]
        token = first_token + i * rows + lax.broadcasted_iota(jnp.int32, (rows, 1), 0)
        token = jnp.where(token >= CONTEXT, token - CONTEXT, token)
        angle = token.astype(f32) * rate
        place = jnp.where(h * quarter < half_width, jnp.sin(angle), jnp.cos(angle))
        stem[h, i * rows : (i + 1) * rows, :] = (gelu(acc + vec_ref[3:4, 0:quarter]) + place).astype(bf16)

    x_peer = lax.rem(h + 2, 4)
    far = lax.rem(core_peer + 2, 4)
    start(None, remote(stem.at[h], stem.at[h], st_s.at[0], st_r.at[0], "head", x_peer))
    start(None, remote(stem.at[h], stem.at[h], st_s.at[1], st_r.at[1], "head", core_peer))
    for p in (3, 4):
        for k in range(3, nz):
            relay(p, k)
    remote(stem.at[x_peer], stem.at[x_peer], st_s.at[0], st_r.at[0], "head", x_peer).wait_recv()
    start(None, remote(stem.at[x_peer], stem.at[x_peer], st_s.at[2], st_r.at[2], "head", core_peer))
    remote(stem.at[core_peer], stem.at[core_peer], st_s.at[1], st_r.at[1], "head", core_peer).wait_recv()
    remote(stem.at[far], stem.at[far], st_s.at[2], st_r.at[2], "head", core_peer).wait_recv()
    for p in (3, 4):
        finish(p)

    def project(i, c):
        at = pl.ds(pl.multiple_of(i * rows, rows), rows)
        parts = [stem[j, at, :].astype(f32) for j in range(4)]
        mean = sum(jnp.sum(v, axis=1, keepdims=True) for v in parts) / width_all
        parts = [v - mean for v in parts]
        var = sum(jnp.sum(v * v, axis=1, keepdims=True) for v in parts) / width_all
        scale = lax.rsqrt(var + 1e-05)
        acc = None
        for j in range(4):
            lanes = slice(j * quarter, (j + 1) * quarter)
            normed = (parts[j] * scale * vec_ref[1:2, lanes] + vec_ref[2:3, lanes]).astype(bf16)
            term = jnp.dot(normed, wqg[lanes, :], preferred_element_type=f32)
            acc = term if acc is None else acc + term
        out_ref[at, :] = acc.astype(bf16)
        return c

    lax.fori_loop(0, toks // rows, project, 0)

    for cond, copy in pending:
        if cond is None:
            copy.wait_send()
        else:
            pl.when(cond)(copy.wait_send)


def fused_device(
    n, mel_buffer, segment_frames, conv1_weight, conv1_bias, conv2_weight, conv2_bias,
    norm_gain, norm_bias, qkv_weight,
):
    toks = mel_buffer.shape[0] // 4
    taps, mels, width_all = conv1_weight.shape
    depth, quarter = conv2_weight.shape[1:]
    out_cols = qkv_weight.shape[1]
    bf16, f32 = jnp.bfloat16, jnp.float32
    vec = jnp.zeros((), f32)
    rows_of = (conv1_bias, norm_gain, norm_bias, conv2_bias), (segment_frames.astype(f32),)
    for first, group in zip((0, 8), rows_of):
        for j, row in enumerate(group):
            vec = vec + jnp.pad(row[None, :], ((first + j, 15 - first - j), (0, width_all - row.shape[0])))
    vmem = pl.BlockSpec(memory_space=pltpu.VMEM)
    dma = pltpu.SemaphoreType.DMA
    return pl.pallas_call(
        functools.partial(fused_kernel, (n, depth, width_all, quarter)),
        out_shape=jax.ShapeDtypeStruct((toks, out_cols), bf16),
        in_specs=[vmem] * 5,
        out_specs=vmem,
        scratch_shapes=[
            pltpu.VMEM((n, 8, 128), f32),
            pltpu.VMEM((toks, 128), bf16),
            pltpu.VMEM((2, toks, 128), bf16),
            pltpu.VMEM((2, toks, 128), bf16),
            pltpu.VMEM((2, HALO, 128), bf16),
            pltpu.VMEM((HALO, 128), bf16),
            pltpu.VMEM((toks + 2 * HALO, 128), f32),
            pltpu.VMEM((toks + 2 * HALO, 128), f32),
            pltpu.VMEM((toks, 384), bf16),
            pltpu.VMEM((toks + HALO, 384), bf16),
            pltpu.VMEM((toks, width_all), bf16),
            pltpu.VMEM((toks + HALO, width_all), bf16),
            pltpu.VMEM((3, width_all, quarter), bf16),
            pltpu.VMEM((width_all, out_cols), bf16),
            pltpu.VMEM((2 * depth, 128), bf16),
            pltpu.VMEM((n, 2 * depth, 128), bf16),
            pltpu.VMEM((4, toks, quarter), bf16),
            pltpu.VMEM((toks + HALO, quarter), f32),
            dma((n,)), dma((n,)), dma((2,)), dma((2,)), dma((3,)), dma((3,)),
            dma((6, n, 3)), dma((6, n)), dma((6,)), dma((3,)), dma((3,)),
        ],
        compiler_params=pltpu.CompilerParams(
            collective_id=0, has_side_effects=True, vmem_limit_bytes=60 * 1024 * 1024
        ),
    )(
        vec, mel_buffer, conv1_weight.reshape(taps * mels, width_all), conv2_weight, qkv_weight,
    )


def solution(mesh):
    n_seq, n_head = mesh.shape["seq"], mesh.shape["head"]

    def local(*args):
        depth = args[4].shape[1]
        if n_head == 4 and n_seq % 2 == 0 and depth % 32 == 0 and args[4].shape[2] % 128 == 64:
            return fused_device(n_seq, *args)
        return per_device(*args)

    in_specs = (
        P("seq", None),
        P("seq"),
        P(),
        P(),
        P(None, "seq", "head"),
        P("head"),
        P(),
        P(),
        P("seq", "head"),
    )
    out_specs = P("seq", "head")
    return jax.shard_map(
        local, mesh=mesh, in_specs=in_specs, out_specs=out_specs, check_vma=False
    )
```

```python
import functools
import math

import jax
import jax.numpy as jnp
from jax import lax
from jax.experimental import pallas as pl
from jax.experimental.pallas import tpu as pltpu
from jax.sharding import PartitionSpec as P

CONTEXT = 1500


LOG_SCALE = math.log(10000.0)


def prefix(value, axis, join, neutral):
    count, mine = (lax.axis_size(axis), lax.axis_index(axis))
    pieces = lax.all_gather(value, axis)
    running = jnp.full_like(value, 0) + jnp.asarray(neutral, value.dtype)

    def step(position, running):
        longer = join(running, pieces[position])
        return jnp.where(position < mine, longer, running)

    return lax.fori_loop(0, count - 1, step, running)


def from_behind(value, axis, by):
    size = lax.axis_size(axis)
    pairs = [(i, i + by) for i in range(size) if 0 <= i + by < size]
    return lax.ppermute(value, axis, pairs)


def padded(value, sides, width):
    for axis, dim in sides:
        size, length = (lax.axis_size(axis), value.shape[dim])
        up = [(i, (i + 1) % size) for i in range(size - 1)]
        down = [(j, i) for i, j in up]
        last = lax.slice_in_dim(value, length - width, length, axis=dim)
        initial = lax.slice_in_dim(value, 0, width, axis=dim)
        before = lax.ppermute(last, axis, up)
        after = lax.ppermute(initial, axis, down)
        value = jnp.concatenate([before, value, after], axis=dim)
    return value


def sinusoid(token_ids, channel_ids, width_all):
    half_width = width_all // 2
    inv_rate = jnp.exp(
        -(LOG_SCALE / (half_width - 1)) * (channel_ids % half_width).astype(jnp.float32)
    )
    angles = (token_ids % CONTEXT).astype(jnp.float32)[:, None] * inv_rate[None, :]
    return jnp.where(channel_ids[None, :] < half_width, jnp.sin(angles), jnp.cos(angles))


def layer_norm(values, gain, shift):
    widened = values.astype(jnp.float32)
    average = jnp.mean(widened, axis=-1, keepdims=True)
    centered = widened - average
    spread = jnp.mean(centered * centered, axis=-1, keepdims=True)
    return (centered * lax.rsqrt(spread + 1e-05) * gain + shift).astype(jnp.bfloat16)


def add_sum(left, right):
    return left + right


def project_rows(normed, shard_rows):
    return jnp.dot(normed, shard_rows, preferred_element_type=jnp.float32)


def per_device(
    mel_buffer,
    segment_frames,
    conv1_weight,
    conv1_bias,
    conv2_weight,
    conv2_bias,
    norm_gain,
    norm_bias,
    qkv_weight,
):
    frames_dev = mel_buffer.shape[0] // 2
    tok_rows = frames_dev // 2
    width_all = conv1_weight.shape[2]
    seq_place = lax.axis_index("seq")
    head_place = lax.axis_index("head")
    own_count = jnp.sum(segment_frames)
    start_frame = prefix(own_count, "seq", add_sum, jnp.zeros((), jnp.int32))
    displaced = (start_frame - seq_place * frames_dev).astype(jnp.int32)
    tail_rows = lax.dynamic_slice_in_dim(mel_buffer, frames_dev - displaced, frames_dev, 0)
    arrived = from_behind(tail_rows, "seq", 1)
    front_pad = jnp.concatenate([jnp.zeros_like(arrived), mel_buffer[:frames_dev]], axis=0)
    own_rows = lax.dynamic_slice_in_dim(front_pad, frames_dev - displaced, frames_dev, 0)
    row_ids = jnp.arange(frames_dev, dtype=jnp.int32)
    frames = jnp.where((row_ids < displaced)[:, None], arrived, own_rows)
    rimmed = padded(frames, (("seq", 0),), 2)
    running = jnp.zeros((frames_dev + 1, width_all), jnp.float32)
    for k in range(3):
        running = running + jnp.dot(
            rimmed[k : k + frames_dev + 1], conv1_weight[k], preferred_element_type=jnp.float32
        )
    first_layer = jax.nn.gelu(running + conv1_bias, approximate=False).astype(jnp.bfloat16)
    keep_mask = (jnp.arange(frames_dev + 1, dtype=jnp.int32) > 0) | (seq_place > 0)
    first_layer = jnp.where(keep_mask[:, None], first_layer, jnp.zeros_like(first_layer))
    frame_pairs = first_layer[:frames_dev].reshape(tok_rows, 2, width_all)
    later_pairs = first_layer[1:].reshape(tok_rows, 2, width_all)
    conv_taps = (frame_pairs[:, 0], frame_pairs[:, 1], later_pairs[:, 1])
    quarter_width = conv2_weight.shape[2]
    zero_start = jnp.zeros((tok_rows, quarter_width), jnp.float32)
    stem_sum = zero_start
    shard_rows = lax.all_gather(conv2_weight, "seq", axis=1, tiled=True)
    for k in range(3):
        inputs = conv_taps[k]
        stem_sum = stem_sum + jnp.dot(inputs, shard_rows[k], preferred_element_type=jnp.float32)
    token_ids = seq_place * tok_rows + jnp.arange(tok_rows, dtype=jnp.int32)
    channel = head_place * quarter_width + jnp.arange(quarter_width, dtype=jnp.int32)
    features = (
        jax.nn.gelu(stem_sum + conv2_bias, approximate=False)
        + sinusoid(token_ids, channel, width_all)
    ).astype(jnp.bfloat16)
    quarter = lax.all_to_all(features, "head", split_axis=0, concat_axis=1, tiled=True)
    normed = layer_norm(quarter, norm_gain, norm_bias)
    widened_rows = lax.all_gather(qkv_weight, "head", axis=1, tiled=True)
    qkv_part = project_rows(normed, lax.all_gather(widened_rows, "seq", axis=0, tiled=True))
    return lax.all_to_all(
        qkv_part.astype(jnp.bfloat16), "head", split_axis=1, concat_axis=0, tiled=True
    )


MESH = pl.DeviceIdType.MESH
HALO = 16
Y_FIRST = (2,)


def gelu(v):
    return 0.5 * v * (1.0 + lax.erf(v * math.sqrt(0.5)))


def fused_kernel(
    dims, seg_ref, mel_ref, w1_ref, b1_ref, w2_ref, b2_ref, gain_ref, shift_ref, wq_ref,
    out_ref, vec_ref, seg_own, seg_all, tail_send, tail_recv, fr, halo_prev, halo_next, ebuf, obuf, x_even, x_odd,
    f_even, f_odd, w2g, wqg, rest, restg, stem, normed, acc0, acc1, seg_s, seg_r, tail_s, tail_r, halo_s, halo_r,
    w_s, w_r, loc, st_s, st_r,
):
    n, depth, width_all, quarter = dims
    nz = n // 2
    toks = fr.shape[1]
    frames_dev = 2 * toks
    me = lax.axis_index("seq")
    h = lax.axis_index("head")
    z, y = me // 2, me % 2
    partner = z * 2 + (1 - y)
    f32, bf16 = jnp.float32, jnp.bfloat16
    core = h % 2
    core_peer = (h // 2) * 2 + (1 - core)
    count = jnp.sum(seg_ref[...].reshape(1, -1).astype(f32), axis=1, keepdims=True)
    seg_own[...] = jnp.broadcast_to(count, seg_own.shape)
    for j, ref in enumerate((b1_ref, gain_ref, shift_ref)):
        vec_ref[j : j + 1, :] = ref[...].reshape(1, width_all)
    vec_ref[3:4, 0:quarter] = b2_ref[...].reshape(1, quarter)
    pending = []

    def remote(src, dst, ss, rs, axis, peer):
        return pltpu.make_async_remote_copy(
            src_ref=src, dst_ref=dst, send_sem=ss, recv_sem=rs,
            device_id={axis: peer}, device_id_type=MESH,
        )

    def start(cond, copy):
        if cond is None:
            copy.start()
        else:
            pl.when(cond)(copy.start)
        pending.append((cond, copy))

    def both(a, b):
        if a is None:
            return b
        return a if b is None else jnp.logical_and(a, b)

    barrier = pltpu.get_barrier_semaphore()
    for p in range(1, n):
        pl.semaphore_signal(
            barrier, inc=1, device_id={"seq": lax.rem(me + p, n)}, device_id_type=MESH
        )
    for p in range(1, 4):
        pl.semaphore_signal(
            barrier, inc=1, device_id={"head": lax.rem(h + p, 4)}, device_id_type=MESH
        )
    half = depth // 2
    out_cols = wqg.shape[1]
    main2, main_q = quarter - 64, out_cols - 64
    rest[0:depth, 0:64] = w2_ref[0, :, main2:]
    rest[0:depth, 64:128] = w2_ref[1, :, main2:]
    rest[depth : depth + half, 0:64] = w2_ref[2, 0:half, main2:]
    rest[depth : depth + half, 64:128] = w2_ref[2, half:, main2:]
    rest[depth + half :, 0:64] = wq_ref[0:half, main_q:]
    rest[depth + half :, 64:128] = wq_ref[half:, main_q:]
    pl.semaphore_wait(barrier, n - 1 + 3)

    for p in range(1, n):
        dst = lax.rem(me + p, n)
        start(None, remote(seg_own, seg_all.at[me], seg_s.at[p], seg_r.at[me], "seq", dst))

    lanes2, lanes_q = pl.ds(0, main2), pl.ds(0, main_q)

    def gathered(p, s):
        if p < 3:
            return w2g.at[p, pl.ds(pl.multiple_of(s * depth, 16), depth), lanes2]
        if p == 5:
            return restg.at[s]
        return wqg.at[pl.ds(pl.multiple_of(s * depth + (p - 3) * half, 16), half), lanes_q]

    def own(p):
        if p == 5:
            return rest
        return w2_ref.at[p, :, lanes2] if p < 3 else wq_ref.at[pl.ds((p - 3) * half, half), lanes_q]

    has_up, has_down = z < nz - 1, z > 0

    def push(cond, p, s, way, mine=False):
        peer = (lax.rem(me + 2, n), lax.rem(me + n - 2, n), partner)[way]
        src = own(p) if mine else gathered(p, s)
        start(cond, remote(src, gathered(p, s), w_s.at[p, s, way], w_r.at[p, s], "seq", peer))

    def arrive(cond, p, s):
        copy = remote(gathered(p, s), gathered(p, s), w_s.at[p, s, 0], w_r.at[p, s], "seq", partner)
        if cond is None:
            copy.wait_recv()
        else:
            pl.when(cond)(copy.wait_recv)

    def start_own(p):
        push(None, p, me, 2, True)
        push(has_up, p, me, 0, True)
        push(has_down, p, me, 1, True)
        pltpu.make_async_copy(own(p), gathered(p, me), loc.at[p]).start()

    def relay_partner(p):
        if p in Y_FIRST:
            arrive(None, p, partner)
            push(has_up, p, partner, 0)
            push(has_down, p, partner, 1)

    def relay(p, k):
        for way in (0, 1):
            valid = z - k >= 0 if way == 0 else z + k <= nz - 1
            onward = has_up if way == 0 else has_down
            shift = -2 * k if way == 0 else 2 * k
            for base in (me, partner) if p in Y_FIRST else (me,):
                s = lax.rem(base + shift + 2 * n, n)
                arrive(valid, p, s)
                push(both(valid, onward), p, s, way)
                if p not in Y_FIRST:
                    push(valid, p, s, 2)

    def finish(p):
        if p not in Y_FIRST:
            for q in range(nz):
                arrive(None, p, 2 * q + (1 - y))
        pltpu.make_async_copy(own(p), gathered(p, me), loc.at[p]).wait()

    early = (2, 5, 0, 1)
    for p in early:
        start_own(p)

    total = jnp.zeros((1, 1), f32)
    for p in range(1, n):
        src = lax.rem(me + n - p, n)
        remote(seg_own, seg_all.at[src], seg_s.at[p], seg_r.at[src], "seq", src).wait_recv()
        total = total + jnp.where(src < me, seg_all[src, 0:1, 0:1], 0.0)
    moved = total.astype(jnp.int32) - me * frames_dev

    rows = 128

    def shifted(first, parity, depth_rows):
        frame = 2 * (first + lax.broadcasted_iota(jnp.int32, (rows, depth_rows), 0)) + parity
        column = lax.broadcasted_iota(jnp.int32, (rows, depth_rows), 1)
        pick = jnp.where(frame - column == moved, 1.0, 0.0).astype(bf16)
        return jnp.dot(pick, mel_ref[:depth_rows, :], preferred_element_type=f32)

    def tail_step(i, c):
        at = pl.multiple_of(i * rows, rows)
        tail_send[pl.ds(at, rows), :] = shifted(toks + at, core, 2 * frames_dev).astype(bf16)
        return c

    lax.fori_loop(0, toks // rows, tail_step, 0)
    tail = remote(tail_send, tail_recv.at[core], tail_s.at[0], tail_r.at[core],
                  "seq", lax.rem(me + 1, n))
    start(me < n - 1, tail)

    relay_partner(2)

    for parity, buf in ((0, ebuf), (1, obuf)):
        def own_step(i, c):
            at = pl.multiple_of(i * rows, rows)
            buf[pl.ds(HALO + at, rows), :] = shifted(at, parity, frames_dev)
            return c
        lax.fori_loop(0, toks // rows, own_step, 0)

    pl.when(me > 0)(tail.wait_recv)
    start(me > 0, remote(tail_recv.at[core], tail_recv.at[core], tail_s.at[1], tail_r.at[core],
                         "head", core_peer))
    pl.when(me > 0)(remote(
        tail_recv.at[1 - core], tail_recv.at[1 - core], tail_s.at[1], tail_r.at[1 - core],
        "head", core_peer).wait_recv)
    for parity, buf in ((0, ebuf), (1, obuf)):
        frame = 2 * lax.broadcasted_iota(jnp.int32, (toks, 128), 0) + parity
        joined = jnp.where(
            frame < moved, tail_recv[parity].astype(f32), buf[HALO : HALO + toks, :])
        buf[HALO : HALO + toks, :] = joined
        fr[parity] = joined.astype(bf16)

    nxt, prv = lax.rem(me + 1, n), lax.rem(me + n - 1, n)
    halos = [
        (me < n - 1, me > 0, fr.at[0, pl.ds(toks - HALO, HALO), :], halo_prev.at[0], nxt),
        (me < n - 1, me > 0, fr.at[1, pl.ds(toks - HALO, HALO), :], halo_prev.at[1], nxt),
        (me > 0, me < n - 1, fr.at[0, pl.ds(0, HALO), :], halo_next, prv),
    ]
    copies = [remote(s, d, halo_s.at[i], halo_r.at[i], "seq", peer)
              for i, (_, _, s, d, peer) in enumerate(halos)]
    for (sends, _, _, _, _), copy in zip(halos, copies):
        start(sends, copy)

    for p in early:
        relay(p, 1)

    x_even[:, 128:256] = fr[0]
    x_even[:, 256:384] = fr[1]

    for (_, takes, _, _, _), copy in zip(halos, copies):
        pl.when(takes)(copy.wait_recv)
    ebuf[0:HALO, :] = jnp.where(me > 0, halo_prev[0].astype(f32), 0.0)
    obuf[0:HALO, :] = jnp.where(me > 0, halo_prev[1].astype(f32), 0.0)
    ebuf[HALO + toks :, :] = jnp.where(me < n - 1, halo_next[...].astype(f32), 0.0)
    x_even[:, 0:128] = obuf[HALO - 1 : HALO - 1 + toks, :].astype(bf16)
    x_odd[:, 0:128] = ebuf[0 : HALO + toks, :].astype(bf16)
    x_odd[:, 128:256] = obuf[0 : HALO + toks, :].astype(bf16)
    x_odd[:, 256:384] = ebuf[1 : HALO + toks + 1, :].astype(bf16)

    start_own(3)
    start_own(4)

    cols = 256

    def even_step(i, c):
        at = pl.ds(pl.multiple_of(i * cols, cols), cols)
        acc = jnp.dot(x_even[...], w1_ref[:, at], preferred_element_type=f32)
        f_even[:, at] = gelu(acc + vec_ref[0:1, at]).astype(bf16)
        return c

    def odd_step(i, c):
        at = pl.ds(pl.multiple_of(i * cols, cols), cols)
        acc = jnp.dot(x_odd[...], w1_ref[:, at], preferred_element_type=f32)
        f_odd[:, at] = gelu(acc + vec_ref[0:1, at]).astype(bf16)
        return c

    lax.fori_loop(0, width_all // cols, even_step, 0)
    for p in early:
        relay(p, 2)
    lax.fori_loop(0, width_all // cols, odd_step, 0)
    keep = jnp.where(me > 0, f_odd[0:HALO, :].astype(f32), 0.0)
    f_odd[0:HALO, :] = keep.astype(bf16)
    for p in (3, 4):
        relay(p, 1)
    for p in early:
        for k in range(3, nz):
            relay(p, k)
    for p in (3, 4):
        relay(p, 2)
    for p in early:
        finish(p)

    for j in range(n):
        at = slice(j * depth, (j + 1) * depth)
        w2g[0, at, main2:] = restg[j, 0:depth, 0:64]
        w2g[1, at, main2:] = restg[j, 0:depth, 64:128]
        w2g[2, j * depth : j * depth + half, main2:] = restg[j, depth : depth + half, 0:64]
        w2g[2, j * depth + half : (j + 1) * depth, main2:] = restg[j, depth : depth + half, 64:128]
        wqg[j * depth : j * depth + half, main_q:] = restg[j, depth + half :, 0:64]
        wqg[j * depth + half : (j + 1) * depth, main_q:] = restg[j, depth + half :, 64:128]

    odd_rows = (HALO + toks) // 3

    def tap_zero(i, c):
        at = pl.ds(pl.multiple_of(i * odd_rows, 16), odd_rows)
        acc0[at, :] = jnp.dot(f_odd[at, :], w2g[0], preferred_element_type=f32)
        return c

    lax.fori_loop(0, 3, tap_zero, 0)
    half_width = width_all // 2
    lane = lax.broadcasted_iota(jnp.int32, (1, quarter), 1) + lax.rem(h * quarter, half_width)
    rate = jnp.exp(-(LOG_SCALE / (half_width - 1)) * lane.astype(f32))
    first_token = lax.rem(me * toks, CONTEXT)
    for i in range(toks // rows):
        acc = jnp.dot(f_even[i * rows : (i + 1) * rows, :], w2g[1], preferred_element_type=f32)
        acc = acc + jnp.dot(
            f_odd[HALO + i * rows : HALO + (i + 1) * rows, :], w2g[2], preferred_element_type=f32)
        acc = acc + acc0[HALO - 1 + i * rows : HALO - 1 + (i + 1) * rows, :]
        token = first_token + i * rows + lax.broadcasted_iota(jnp.int32, (rows, 1), 0)
        token = jnp.where(token >= CONTEXT, token - CONTEXT, token)
        angle = token.astype(f32) * rate
        place = jnp.where(h * quarter < half_width, jnp.sin(angle), jnp.cos(angle))
        stem[h, i * rows : (i + 1) * rows, :] = (gelu(acc + vec_ref[3:4, 0:quarter]) + place).astype(bf16)

    x_peer = lax.rem(h + 2, 4)
    far = lax.rem(core_peer + 2, 4)
    start(None, remote(stem.at[h], stem.at[h], st_s.at[0], st_r.at[0], "head", x_peer))
    start(None, remote(stem.at[h], stem.at[h], st_s.at[1], st_r.at[1], "head", core_peer))
    remote(stem.at[x_peer], stem.at[x_peer], st_s.at[0], st_r.at[0], "head", x_peer).wait_recv()
    start(None, remote(stem.at[x_peer], stem.at[x_peer], st_s.at[2], st_r.at[2], "head", core_peer))
    remote(stem.at[core_peer], stem.at[core_peer], st_s.at[1], st_r.at[1], "head", core_peer).wait_recv()
    remote(stem.at[far], stem.at[far], st_s.at[2], st_r.at[2], "head", core_peer).wait_recv()

    def normalise(i, c):
        at = pl.ds(pl.multiple_of(i * rows, rows), rows)
        parts = [stem[j, at, :].astype(f32) for j in range(4)]
        mean = sum(jnp.sum(v, axis=1, keepdims=True) for v in parts) / width_all
        parts = [v - mean for v in parts]
        var = sum(jnp.sum(v * v, axis=1, keepdims=True) for v in parts) / width_all
        scale = lax.rsqrt(var + 1e-05)
        for j in range(4):
            lanes = slice(j * quarter, (j + 1) * quarter)
            normed[j, at, :] = (
                parts[j] * scale * vec_ref[1:2, lanes] + vec_ref[2:3, lanes]).astype(bf16)
        return c

    lax.fori_loop(0, toks // rows, normalise, 0)
    for p in (3, 4):
        for k in range(3, nz):
            relay(p, k)
        pltpu.make_async_copy(own(p), gathered(p, me), loc.at[p]).wait()

    def group(g, first):
        for p in (3, 4):
            arrive(None, p, 2 * g + (1 - y))
        columns = pl.ds(pl.multiple_of(g * 2 * depth, 2 * depth), 2 * depth)

        def step(i, c):
            at = pl.ds(pl.multiple_of(i * rows, rows), rows)
            term = jnp.dot(normed[g, at, :], wqg[columns, :], preferred_element_type=f32)
            acc1[at, :] = term if first else acc1[at, :] + term
            return c

        lax.fori_loop(0, toks // rows, step, 0)

    group(z, True)
    for k in range(1, nz):
        pl.when(z - k >= 0)(functools.partial(group, jnp.maximum(z - k, 0), False))
        pl.when(z + k <= nz - 1)(functools.partial(group, jnp.minimum(z + k, nz - 1), False))
    out_ref[...] = acc1[...].astype(bf16)

    for cond, copy in pending:
        if cond is None:
            copy.wait_send()
        else:
            pl.when(cond)(copy.wait_send)


def fused_device(
    n, mel_buffer, segment_frames, conv1_weight, conv1_bias, conv2_weight, conv2_bias,
    norm_gain, norm_bias, qkv_weight,
):
    toks = mel_buffer.shape[0] // 4
    taps, mels, width_all = conv1_weight.shape
    depth, quarter = conv2_weight.shape[1:]
    out_cols = qkv_weight.shape[1]
    bf16, f32 = jnp.bfloat16, jnp.float32
    vmem = pl.BlockSpec(memory_space=pltpu.VMEM)
    dma = pltpu.SemaphoreType.DMA
    return pl.pallas_call(
        functools.partial(fused_kernel, (n, depth, width_all, quarter)),
        out_shape=jax.ShapeDtypeStruct((toks, out_cols), bf16),
        in_specs=[vmem] * 9,
        out_specs=vmem,
        scratch_shapes=[
            pltpu.VMEM((8, width_all), f32),
            pltpu.VMEM((8, 128), f32),
            pltpu.VMEM((n, 8, 128), f32),
            pltpu.VMEM((toks, 128), bf16),
            pltpu.VMEM((2, toks, 128), bf16),
            pltpu.VMEM((2, toks, 128), bf16),
            pltpu.VMEM((2, HALO, 128), bf16),
            pltpu.VMEM((HALO, 128), bf16),
            pltpu.VMEM((toks + 2 * HALO, 128), f32),
            pltpu.VMEM((toks + 2 * HALO, 128), f32),
            pltpu.VMEM((toks, 384), bf16),
            pltpu.VMEM((toks + HALO, 384), bf16),
            pltpu.VMEM((toks, width_all), bf16),
            pltpu.VMEM((toks + HALO, width_all), bf16),
            pltpu.VMEM((3, width_all, quarter), bf16),
            pltpu.VMEM((width_all, out_cols), bf16),
            pltpu.VMEM((2 * depth, 128), bf16),
            pltpu.VMEM((n, 2 * depth, 128), bf16),
            pltpu.VMEM((4, toks, quarter), bf16),
            pltpu.VMEM((4, toks, quarter), bf16),
            pltpu.VMEM((toks + HALO, quarter), f32),
            pltpu.VMEM((toks, out_cols), f32),
            dma((n,)), dma((n,)), dma((2,)), dma((2,)), dma((3,)), dma((3,)),
            dma((6, n, 3)), dma((6, n)), dma((6,)), dma((3,)), dma((3,)),
        ],
        compiler_params=pltpu.CompilerParams(
            collective_id=0, has_side_effects=True, vmem_limit_bytes=60 * 1024 * 1024
        ),
    )(
        segment_frames, mel_buffer, conv1_weight.reshape(taps * mels, width_all), conv1_bias,
        conv2_weight, conv2_bias, norm_gain, norm_bias, qkv_weight,
    )


def solution(mesh):
    n_seq, n_head = mesh.shape["seq"], mesh.shape["head"]

    def local(*args):
        depth = args[4].shape[1]
        if n_head == 4 and n_seq == 8 and depth % 32 == 0 and args[4].shape[2] % 128 == 64:
            return fused_device(n_seq, *args)
        return per_device(*args)

    in_specs = (
        P("seq", None),
        P("seq"),
        P(),
        P(),
        P(None, "seq", "head"),
        P("head"),
        P(),
        P(),
        P("seq", "head"),
    )
    out_specs = P("seq", "head")
    return jax.shard_map(
        local, mesh=mesh, in_specs=in_specs, out_specs=out_specs, check_vma=False
    )
```
